32 devices in a mesh: expert: 16 (over z, y, x), col: 2 (over core).
Axes of the slice: x: 2, y: 2, z: 4, core: 2. Of those that a mesh axis runs over, the one named last changes fastest.
Arguments:
- out_grads: bfloat16 [2048, 8, 1024], P(('expert', 'col')), may hold values from -4 to 4
- expert_ids: int32 [2048, 8], P(('expert', 'col')), may hold values from 0 to 15, all different within a row; in each aligned block of 64 rows (0 to 63, 64 to 127, ...) at most 64 rows name the same one
- damping: float32 [16], P('expert'), may hold values from 0.5 to 1.5
- expert_grad: bfloat16 [16, 1024, 3584], P('expert', None, 'col'), may hold values from -6 to 6
Outputs:
- preconditioned: bfloat16 [16, 1024, 3584], P('expert', None, 'col')
The draws below stay inside these ranges and needn't reach their ends.
Inputs may be any that keep to these rules, and one draw needn't show every extreme that they name: `expert_ids`: each row names 8 different experts; within the 64 rows of one device no expert is named by more than 64 rows, and every expert is named somewhere.
All inputs are finite; a program needn't handle non-finite values.
Results may differ from the reference program's by a relative error of at most 0.0051.
Values may be sent and summed in bfloat16 or wider, within the bound.
No kernel may reach another device: no remote copies, remote signals or barrier semaphores. Data moves between devices by JAX's collectives and lax.ppermute only.
A program may use at most 128 MiB of HBM per device.

```python
import math
import jax
import jax.numpy as jnp
import numpy as np
from jax import lax

FFW = 1024
DW = 3584
TOP = 8
TOK_DEV = 64
EXPERTS = 16
CAP = 64
ROW_SCALE = 1024
TOKENS = 2048
N_EXPERT = 16
N_COL = 2


def draw_out_grads(key, part):
    first_key = jax.random.fold_in(key, 11)
    values = jnp.clip(jax.random.normal(first_key, (TOKENS, TOP, FFW), jnp.float32), -4.0, 4.0)
    return values.astype(jnp.bfloat16)


def steps_of(key, extent, cuts, smallest, high):
    def one(dim, shards_of):
        steps = jax.random.uniform(jax.random.fold_in(jax.random.fold_in(key, 6), dim), (shards_of,), jnp.float32, smallest / len(cuts), high / len(cuts))
        return jnp.repeat(jnp.exp(steps), extent[dim] // shards_of).reshape((-1,) + (1,) * (len(extent) - dim - 1))

    factor_of = one(*cuts[0])
    for cut in cuts[1:]:
        factor_of = factor_of * one(*cut)
    return factor_of


def assign_block(rng, own, number, rows, number_of, top, limit, skew):
    ranking = jax.random.permutation(rng, number_of)
    crowded, ordinary = portions_of(number_of, rows * top, limit, skew, True), portions_of(number_of, rows * top, limit, skew, False)
    places = jnp.arange(number_of)

    def named(sizes, rotation):
        used = int((sizes > 0).sum())
        fixed = max(1, used // 4)
        passed = fixed + (places - fixed + rotation * (used - fixed)) % max(1, number_of - fixed)
        return jnp.zeros((number_of,), jnp.int32).at[ranking[jnp.where(places < fixed, places, passed)]].set(jnp.asarray(sizes, jnp.int32))

    sizes = jnp.where(number % 4 == 0, named(crowded, number // 4), named(ordinary, number - number // 4 - 1))
    mixed = jax.random.permutation(jax.random.fold_in(own, 3), number_of)
    giver, sink = mixed[0:number_of // 2 * 2:2], mixed[1:number_of // 2 * 2:2]
    slack = jnp.minimum(sizes[giver] - 1, limit - sizes[sink]) // 2
    slack = jnp.where((giver == ranking[0]) | (sink == ranking[0]) | (sizes[sink] == 0), 0, jnp.maximum(slack, 0))
    passed = jax.random.randint(jax.random.fold_in(own, 4), (number_of // 2,), 0, 1 << 20) % (slack + 1)
    sizes = sizes.at[giver].add(-passed).at[sink].add(passed)
    labels = jnp.searchsorted(jnp.cumsum(sizes), jnp.arange(rows * top), side="right").astype(jnp.int32)
    listing = labels.reshape(top, rows).T
    listing = listing[jax.random.permutation(jax.random.fold_in(own, 1), rows)]
    rotation = jax.random.randint(jax.random.fold_in(own, 2), (rows, 1), 0, top)
    return jnp.take_along_axis(listing, (jnp.arange(top)[None, :] + rotation) % top, axis=1)


def portions_of(number_of, total, bound, skew, full):
    weights = [(1 << 20) // math.isqrt(grade ** skew) + 1 for grade in range(1, number_of + 1)]
    largest = bound if full else min(bound, max(-(-total // number_of), total * weights[0] // sum(weights)))
    least = 1 if total - largest >= number_of - 1 else 0
    given, rest = [largest] + [least] * (number_of - 1), total - largest - least * (number_of - 1)
    while rest > 0:
        movable = [i for i in range(1, number_of) if given[i] < largest] or [i for i in range(1, number_of) if given[i] < bound]
        whole, left = sum([weights[i] for i in movable]), rest
        for i in movable:
            extra = min(bound - given[i], max(1, left * weights[i] // whole), rest)
            given[i] = given[i] + extra
            rest = rest - extra
    return np.array(given)


def gaussian(own_key, dims, width, limit, pieces=(), kind=jnp.bfloat16):
    values = jax.random.normal(own_key, dims, jnp.float32) * width
    if len(pieces) > 0:
        values = steps_of(own_key, dims, pieces, -0.22, 0.18) * values
    return jnp.clip(values, min=-limit, max=limit).astype(kind)


def setup_inputs(seed: int = 0) -> dict:
    streams_of = jax.random.split(jax.random.key(seed), 5)
    out_grads = draw_out_grads(jax.random.fold_in(streams_of[4], 71), 0)
    expert_ids_keys = jax.random.split(jax.random.fold_in(streams_of[1], 1), TOKENS // TOK_DEV)
    expert_ids_turns = jax.random.permutation(jax.random.fold_in(streams_of[1], 3), TOKENS // TOK_DEV)
    expert_ids = jax.vmap(lambda own, number: assign_block(jax.random.fold_in(streams_of[1], 2), own, number, TOK_DEV, EXPERTS, TOP, CAP, 2))(expert_ids_keys, expert_ids_turns).reshape((TOKENS, TOP))
    damping = jnp.clip(jnp.exp(math.log(1.5) - 1.0986123 * jax.random.uniform(streams_of[2], (EXPERTS,), jnp.float32) ** steps_of(streams_of[2], (EXPERTS,), ((0, 16),), -0.2, 0.2)), 0.5, 1.5)
    expert_grad = gaussian(streams_of[3], (EXPERTS, FFW, DW), 1.0, 6.0, ((0, 16), (2, 2)))
    return dict(out_grads=out_grads, expert_ids=expert_ids, damping=damping, expert_grad=expert_grad)


def reference(out_grads, expert_ids, damping, expert_grad):
    sources = N_EXPERT * N_COL
    per_source = TOK_DEV * TOP
    hidden_width = out_grads.shape[-1]
    source_ids = expert_ids.reshape(sources, per_source)
    onehot = (source_ids[:, :, None] == jnp.arange(EXPERTS, dtype=jnp.int32)[None, None, :]).astype(jnp.int32)
    before = jnp.cumsum(onehot, axis=1) - onehot
    slot_index = jnp.sum(before * onehot, axis=2).astype(jnp.int32)
    target = (source_ids * CAP + slot_index).astype(jnp.int32)
    source_rows = out_grads.reshape(sources, per_source, hidden_width)

    def place(where, values):
        return jnp.zeros((EXPERTS * CAP, hidden_width), out_grads.dtype).at[where].set(values)
    buffer = jax.vmap(place)(target, source_rows).reshape(sources, EXPERTS, CAP, hidden_width)
    identity = jnp.eye(hidden_width, dtype=jnp.float32)

    def one_expert(index):
        block_rows = lax.dynamic_index_in_dim(buffer, index, 1, keepdims=False).reshape(-1, hidden_width)
        gram = lax.dot_general(block_rows.astype(jnp.float32), block_rows.astype(jnp.float32), (((0,), (0,)), ((), ())), preferred_element_type=jnp.float32)
        damp_value = lax.dynamic_index_in_dim(damping, index, 0, keepdims=False)
        factor = gram / ROW_SCALE + damp_value * identity
        lower_factor = jnp.linalg.cholesky(factor)
        inverse = jax.scipy.linalg.cho_solve((lower_factor, True), identity).astype(jnp.bfloat16)
        gradient = lax.dynamic_index_in_dim(expert_grad, index, 0, keepdims=False)
        return jnp.dot(inverse.astype(jnp.float32), gradient.astype(jnp.float32), preferred_element_type=jnp.float32).astype(jnp.bfloat16)
    return lax.map(one_expert, jnp.arange(EXPERTS, dtype=jnp.int32))
```

```python
import functools

import jax
import jax.numpy as jnp
from jax import lax
from jax.experimental import pallas as pl
from jax.experimental.pallas import tpu as pltpu
from jax.sharding import PartitionSpec as P

F32 = jnp.float32
BF16 = jnp.bfloat16
NN = (((1,), (0,)), ((), ()))
NT = (((1,), (1,)), ((), ()))
TN = (((0,), (0,)), ((), ()))

SPLIT_LIMIT = 512.0
ENOUGH = 1.0e5


def mul(a, b, dims=NN):
    return lax.dot_general(a, b, dims, preferred_element_type=F32)


def split(x):
    high = x.astype(BF16)
    return high, (x - high.astype(F32)).astype(BF16)


def left_of(x):
    high, low = split(x)
    return jnp.concatenate([high, low, high], axis=1)


def right_of(x):
    high, low = split(x)
    return jnp.concatenate([high, high, low], axis=0)


def right_transposed_of(x):
    high, low = split(x)
    return jnp.concatenate([high, high, low], axis=1)


def factor_kernel(block, row_scale, damping_ref, own_ref, other_ref, grad_hbm, out_hbm,
                  state, inverse, grad, out, pair, grad_sem, out_sem):
    width = state.shape[0]
    count = width // block
    columns = grad.shape[1]
    step = 256 if columns % 256 == 0 else 128
    pltpu.make_async_copy(grad_hbm, grad, grad_sem).start()
    damp = damping_ref[0]

    def span(i):
        return slice(i * block, (i + 1) * block)

    row = lax.broadcasted_iota(jnp.int32, (block, block), 0)
    col = lax.broadcasted_iota(jnp.int32, (block, block), 1)
    identity = jnp.where(row == col, 1.0, 0.0).astype(F32)

    block_bound = jnp.float32(0.0)
    row_bound = [jnp.float32(0.0) for _ in range(count)]
    for i in range(count):
        for j in range(i + 1):
            gram = mul(own_ref[:, span(i)], own_ref[:, span(j)], TN)
            gram += mul(other_ref[:, span(i)], other_ref[:, span(j)], TN)
            piece = gram / row_scale
            if i == j:
                piece += damp * identity
            state[span(i), span(j)] = piece
            size = jnp.abs(piece)
            by_row = jnp.max(jnp.sum(size, axis=1, keepdims=True))
            row_bound[i] += by_row
            if i == j:
                block_bound = jnp.maximum(block_bound, by_row)
            else:
                row_bound[j] += jnp.max(jnp.sum(size, axis=0, keepdims=True))
    full_bound = functools.reduce(jnp.maximum, row_bound)
    well = full_bound <= SPLIT_LIMIT * damp

    @pl.when(well)
    def _():
        upper = jnp.full((8, 128), block_bound, F32)
        lower = jnp.full((8, 128), damp, F32)
        scale = jnp.max(2.0 / (upper + lower))
        start = jnp.max((upper + lower) / jnp.maximum(upper - lower, 1e-3 * upper))

        def longer(carry):
            return carry[0] < ENOUGH

        def double(carry):
            return 2.0 * carry[0] * carry[0] - 1.0, carry[1] + 1

        _, doublings = lax.while_loop(longer, double, (start, jnp.int32(0)))
        doublings = jnp.maximum(doublings, 2)

        def after(tau):
            following = 2.0 * tau * tau - 1.0
            inverted = jnp.max(1.0 / jnp.full((8, 128), following, F32))
            return following, 2.0 * tau * tau * inverted, inverted

        for k in range(count):
            residual = identity - scale * state[span(k), span(k)]
            tau, gain, shift = after(start)
            pair[0:block, :] = (gain * scale) * (identity + residual)
            pair[block:, :] = gain * mul(left_of(residual), right_of(residual)) - shift * identity

            def level(_, tau):
                tau, gain, shift = after(tau)
                both = pair[...]
                product = gain * mul(left_of(both), right_of(both[block:, :]))
                pair[0:block, :] = gain * both[0:block, :] + product[0:block, :]
                pair[block:, :] = product[block:, :] - shift * identity
                return tau

            tau = lax.fori_loop(0, doublings - 2, level, tau)
            _, gain, _ = after(tau)
            guess = pair[0:block, :]
            pivot = gain * (guess + mul(left_of(guess), right_of(pair[block:, :])))

            before, behind = range(k), range(k + 1, count)
            left = {i: left_of(state[span(k), span(i)].T) for i in before}
            for i in behind:
                left[i] = left_of(state[span(i), span(k)])
            turned = {}
            if k:
                pivot_left = left_of(pivot)
                for j in before:
                    value = mul(pivot_left, right_of(state[span(k), span(j)]))
                    turned[j] = right_of(value)
                    state[span(k), span(j)] = value
            pivot_right = right_of(pivot)
            flat = {j: right_transposed_of(state[span(j), span(k)]) for j in behind}
            for i in behind:
                value = mul(left[i], pivot_right)
                state[span(i), span(k)] = value
                straight = left_of(value)
                for j in range(k + 1, i + 1):
                    state[span(i), span(j)] -= mul(straight, flat[j], NT)
            for i in list(before) + list(behind):
                for j in before:
                    if j <= i:
                        state[span(i), span(j)] -= mul(left[i], turned[j])
            state[span(k), span(k)] = -pivot

        for i in range(count):
            for j in range(i + 1):
                piece = -state[span(i), span(j)]
                inverse[span(i), span(j)] = piece.astype(BF16)
                if i != j:
                    inverse[span(j), span(i)] = piece.T.astype(BF16)

    @pl.when(jnp.logical_not(well))
    def _():
        for i in range(count):
            for j in range(i):
                state[span(j), span(i)] = state[span(i), span(j)].T
        lanes = lax.broadcasted_iota(jnp.int32, (1, width), 1)
        tile_lanes = lax.broadcasted_iota(jnp.int32, (1, 128), 1)

        def sweep(k, _):
            tile = pl.multiple_of((k // 128) * 128, 128)
            line = state[pl.ds(k, 1), :]
            here = lanes == k
            scale = 1.0 / jnp.sum(jnp.where(here, line, 0.0), axis=1, keepdims=True)
            scaled = line * scale

            def strip(r, _):
                rows = pl.ds(pl.multiple_of(r * 128, 128), 128)
                mine = jnp.sum(
                    jnp.where(tile_lanes == k - tile, state[rows, pl.ds(tile, 128)], 0.0),
                    axis=1, keepdims=True)
                strip_value = state[rows, :]
                swept = jnp.where(here, mine * scale, strip_value - mine * scaled)
                state[rows, :] = swept
                return 0

            lax.fori_loop(0, width // 128, strip, 0)
            state[pl.ds(k, 1), :] = jnp.where(here, -scale, scaled)
            return 0

        lax.fori_loop(0, width, sweep, 0)
        for i in range(count):
            inverse[span(i), :] = (-state[span(i), :]).astype(BF16)

    pltpu.make_async_copy(grad_hbm, grad, grad_sem).wait()
    for c in range(columns // step):
        part = slice(c * step, (c + 1) * step)
        out[:, part] = mul(inverse[...], grad[:, part]).astype(BF16)
        pltpu.make_async_copy(out.at[:, part], out_hbm.at[:, part], out_sem.at[c]).start()
    for c in range(columns // step):
        part = slice(c * step, (c + 1) * step)
        pltpu.make_async_copy(out.at[:, part], out_hbm.at[:, part], out_sem.at[c]).wait()


def precondition(damping, own, other, gradient, row_scale):
    width, columns = gradient.shape
    block = 256 if width % 256 == 0 else 128
    vmem = pl.BlockSpec(memory_space=pltpu.VMEM)
    hbm = pl.BlockSpec(memory_space=pl.ANY)
    step = 256 if columns % 256 == 0 else 128
    return pl.pallas_call(
        functools.partial(factor_kernel, block, float(row_scale)),
        out_shape=jax.ShapeDtypeStruct((width, columns), BF16),
        in_specs=[pl.BlockSpec(memory_space=pltpu.SMEM), vmem, vmem, hbm],
        out_specs=hbm,
        scratch_shapes=[
            pltpu.VMEM((width, width), F32),
            pltpu.VMEM((width, width), BF16),
            pltpu.VMEM((width, columns), BF16),
            pltpu.VMEM((width, columns), BF16),
            pltpu.VMEM((2 * block, block), F32),
            pltpu.SemaphoreType.DMA,
            pltpu.SemaphoreType.DMA((columns // step,)),
        ],
        compiler_params=pltpu.CompilerParams(vmem_limit_bytes=60000 * 1024),
        name="precondition",
    )(damping, own, other, gradient)


def on_device(out_grads, expert_ids, damping, expert_grad):
    tokens_here, top_count, hidden_width = out_grads.shape
    groups = lax.axis_size("expert")
    replicas = lax.axis_size("col")
    capacity = min(tokens_here, max(2, 2 * tokens_here * top_count // groups))
    flat_ids = expert_ids.reshape(-1)
    onehot = (flat_ids[:, None] == jnp.arange(groups, dtype=jnp.int32)[None, :]).astype(jnp.int32)
    before = jnp.cumsum(onehot, axis=0) - onehot
    slot_index = jnp.sum(before * onehot, axis=1)
    target = flat_ids * capacity + slot_index
    outgoing = (
        jnp.zeros((groups * capacity, hidden_width), out_grads.dtype)
        .at[target]
        .set(out_grads.reshape(-1, hidden_width))
    )
    arrived = lax.all_to_all(
        outgoing.reshape(groups, capacity, hidden_width),
        "expert",
        split_axis=0,
        concat_axis=0,
        tiled=True,
    ).reshape(groups * capacity, hidden_width)
    other = lax.ppermute(arrived, "col", [(0, 1), (1, 0)])
    row_scale = tokens_here * top_count * replicas
    return precondition(damping, arrived, other, expert_grad[0], row_scale)[None]


def solution(mesh):
    in_specs = (
        P(("expert", "col"), None, None),
        P(("expert", "col"), None),
        P("expert"),
        P("expert", None, "col"),
    )
    out_specs = P("expert", None, "col")
    return jax.shard_map(
        on_device, mesh=mesh, in_specs=in_specs, out_specs=out_specs, check_vma=False
    )
```

```python
import functools

import jax
import jax.numpy as jnp
from jax import lax
from jax.experimental import pallas as pl
from jax.experimental.pallas import tpu as pltpu
from jax.sharding import PartitionSpec as P


F32 = jnp.float32
BF16 = jnp.bfloat16
NN = (((1,), (0,)), ((), ()))
NT = (((1,), (1,)), ((), ()))
TN = (((0,), (0,)), ((), ()))

SPLIT_LIMIT = 512.0
ENOUGH = 1.0e5


def mul(a, b, dims=NN):
    return lax.dot_general(a, b, dims, preferred_element_type=F32)


def split(x):
    high = x.astype(BF16)
    return high, (x - high.astype(F32)).astype(BF16)


def left_of(x):
    high, low = split(x)
    return jnp.concatenate([high, low, high], axis=1)


def right_of(x):
    high, low = split(x)
    return jnp.concatenate([high, high, low], axis=0)


def right_transposed_of(x):
    high, low = split(x)
    return jnp.concatenate([high, high, low], axis=1)


def add_gram(block, rows, state, partial):
    width = state.shape[1]
    for i in range(width // block):
        across, down = (i + 1) * block, slice(i * block, (i + 1) * block)
        value = mul(rows[:, down], rows[:, :across], TN)
        if partial is not None:
            value += partial[down, :across]
        state[down, :across] = value


def gram_kernel(block, pieces, *refs):
    rows = jnp.concatenate([ref[...] for ref in refs[:pieces]], axis=0)
    partial = refs[pieces] if len(refs) > pieces + 1 else None
    add_gram(block, rows, refs[-1], partial)


def dispatch_kernel(offsets, experts_of, flat_ids_ref, rows_ref, *out_refs):
    top, tokens = flat_ids_ref.shape
    entries = top * tokens
    me = lax.axis_index("expert")
    token_of = lax.broadcasted_iota(jnp.int32, (tokens, entries), 1) // top
    spread = (token_of == lax.broadcasted_iota(jnp.int32, (tokens, entries), 0)).astype(F32)
    named = lax.dot_general(flat_ids_ref[...].astype(F32), spread, NN,
                            precision=lax.Precision.HIGHEST, preferred_element_type=F32)
    slot = lax.broadcasted_iota(jnp.int32, (top, entries), 1) % top
    mine = slot == lax.broadcasted_iota(jnp.int32, (top, entries), 0)
    ids = jnp.sum(jnp.where(mine, named, 0.0), axis=0, keepdims=True)
    group = 16
    span = group * top
    for start in range(0, tokens, group):
        here = ids[:, start * top:start * top + span]
        token = lax.broadcasted_iota(jnp.int32, (group, span), 1) // top
        same = token == lax.broadcasted_iota(jnp.int32, (group, span), 0)
        picks = []
        for offset in offsets:
            expert = experts_of(me, offset).astype(F32)
            picks.append(jnp.where(same & (here == expert), 1.0, 0.0).astype(BF16))
        moved = mul(jnp.concatenate(picks, axis=0), rows_ref[start * top:start * top + span, :])
        for n, ref in enumerate(out_refs):
            ref[start:start + group, :] = moved[n * group:(n + 1) * group, :].astype(BF16)


def factor_kernel(block, row_scale, pieces, damping_ref, partial_ref, *refs):
    row_refs, refs = refs[:pieces], refs[pieces:]
    grad_hbm, out_hbm, state, inverse, grad, out, pair, grad_sem, out_sem = refs
    width = state.shape[0]
    count = width // block
    columns = grad.shape[1]
    step = 256 if columns % 256 == 0 else 128
    pltpu.make_async_copy(grad_hbm, grad, grad_sem).start()
    damp = damping_ref[0]

    def span(i):
        return slice(i * block, (i + 1) * block)

    row = lax.broadcasted_iota(jnp.int32, (block, block), 0)
    col = lax.broadcasted_iota(jnp.int32, (block, block), 1)
    identity = jnp.where(row == col, 1.0, 0.0).astype(F32)

    rows = jnp.concatenate([ref[...] for ref in row_refs], axis=0)
    add_gram(block, rows, state, partial_ref)
    block_bound = jnp.float32(0.0)
    row_bound = [jnp.float32(0.0) for _ in range(count)]
    for i in range(count):
        for j in range(i + 1):
            piece = state[span(i), span(j)] / row_scale
            if i == j:
                piece += damp * identity
            state[span(i), span(j)] = piece
            size = jnp.abs(piece)
            by_row = jnp.max(jnp.sum(size, axis=1, keepdims=True))
            row_bound[i] += by_row
            if i == j:
                block_bound = jnp.maximum(block_bound, by_row)
            else:
                row_bound[j] += jnp.max(jnp.sum(size, axis=0, keepdims=True))
    full_bound = functools.reduce(jnp.maximum, row_bound)
    well = full_bound <= SPLIT_LIMIT * damp

    @pl.when(well)
    def _():
        upper = jnp.full((8, 128), block_bound, F32)
        lower = jnp.full((8, 128), damp, F32)
        scale = jnp.max(2.0 / (upper + lower))
        start = jnp.max((upper + lower) / jnp.maximum(upper - lower, 1e-3 * upper))

        def longer(carry):
            return carry[0] < ENOUGH

        def double(carry):
            return 2.0 * carry[0] * carry[0] - 1.0, carry[1] + 1

        _, doublings = lax.while_loop(longer, double, (start, jnp.int32(0)))
        doublings = jnp.maximum(doublings, 2)

        def after(tau):
            following = 2.0 * tau * tau - 1.0
            inverted = jnp.max(1.0 / jnp.full((8, 128), following, F32))
            return following, 2.0 * tau * tau * inverted, inverted

        for k in range(count):
            residual = identity - scale * state[span(k), span(k)]
            tau, gain, shift = after(start)
            pair[0:block, :] = (gain * scale) * (identity + residual)
            pair[block:, :] = gain * mul(left_of(residual), right_of(residual)) - shift * identity

            def level(_, tau):
                tau, gain, shift = after(tau)
                both = pair[...]
                product = gain * mul(left_of(both), right_of(both[block:, :]))
                pair[0:block, :] = gain * both[0:block, :] + product[0:block, :]
                pair[block:, :] = product[block:, :] - shift * identity
                return tau

            tau = lax.fori_loop(0, doublings - 2, level, tau)
            _, gain, _ = after(tau)
            guess = pair[0:block, :]
            pivot = gain * (guess + mul(left_of(guess), right_of(pair[block:, :])))

            before, behind = range(k), range(k + 1, count)
            left = {i: left_of(state[span(k), span(i)].T) for i in before}
            for i in behind:
                left[i] = left_of(state[span(i), span(k)])
            turned = {}
            if k:
                pivot_left = left_of(pivot)
                for j in before:
                    value = mul(pivot_left, right_of(state[span(k), span(j)]))
                    turned[j] = right_of(value)
                    state[span(k), span(j)] = value
            pivot_right = right_of(pivot)
            flat = {j: right_transposed_of(state[span(j), span(k)]) for j in behind}
            for i in behind:
                value = mul(left[i], pivot_right)
                state[span(i), span(k)] = value
                straight = left_of(value)
                for j in range(k + 1, i + 1):
                    state[span(i), span(j)] -= mul(straight, flat[j], NT)
            for i in list(before) + list(behind):
                for j in before:
                    if j <= i:
                        state[span(i), span(j)] -= mul(left[i], turned[j])
            state[span(k), span(k)] = -pivot

        for i in range(count):
            for j in range(i + 1):
                piece = -state[span(i), span(j)]
                inverse[span(i), span(j)] = piece.astype(BF16)
                if i != j:
                    inverse[span(j), span(i)] = piece.T.astype(BF16)

    @pl.when(jnp.logical_not(well))
    def _():
        for i in range(count):
            for j in range(i):
                state[span(j), span(i)] = state[span(i), span(j)].T
        lanes = lax.broadcasted_iota(jnp.int32, (1, width), 1)
        tile_lanes = lax.broadcasted_iota(jnp.int32, (1, 128), 1)

        def sweep(k, _):
            tile = pl.multiple_of((k // 128) * 128, 128)
            line = state[pl.ds(k, 1), :]
            here = lanes == k
            scale = 1.0 / jnp.sum(jnp.where(here, line, 0.0), axis=1, keepdims=True)
            scaled = line * scale

            def strip(r, _):
                rows = pl.ds(pl.multiple_of(r * 128, 128), 128)
                mine = jnp.sum(
                    jnp.where(tile_lanes == k - tile, state[rows, pl.ds(tile, 128)], 0.0),
                    axis=1, keepdims=True)
                strip_value = state[rows, :]
                swept = jnp.where(here, mine * scale, strip_value - mine * scaled)
                state[rows, :] = swept
                return 0

            lax.fori_loop(0, width // 128, strip, 0)
            state[pl.ds(k, 1), :] = jnp.where(here, -scale, scaled)
            return 0

        lax.fori_loop(0, width, sweep, 0)
        for i in range(count):
            inverse[span(i), :] = (-state[span(i), :]).astype(BF16)

    pltpu.make_async_copy(grad_hbm, grad, grad_sem).wait()
    for c in range(columns // step):
        part = slice(c * step, (c + 1) * step)
        out[:, part] = mul(inverse[...], grad[:, part]).astype(BF16)
        pltpu.make_async_copy(out.at[:, part], out_hbm.at[:, part], out_sem.at[c]).start()
    for c in range(columns // step):
        part = slice(c * step, (c + 1) * step)
        pltpu.make_async_copy(out.at[:, part], out_hbm.at[:, part], out_sem.at[c]).wait()


def block_of(width):
    return 256 if width % 256 == 0 else 128


VMEM = pl.BlockSpec(memory_space=pltpu.VMEM)
BIG = pltpu.CompilerParams(vmem_limit_bytes=36 * 2**20)
SMALL = pltpu.CompilerParams(vmem_limit_bytes=20 * 2**20)


def partial_gram(pieces, partial=None):
    width = pieces[0].shape[1]
    total = sum(piece.shape[0] for piece in pieces)
    operands = list(pieces) + ([] if partial is None else [partial])
    return pl.pallas_call(
        functools.partial(gram_kernel, block_of(width), len(pieces)),
        out_shape=jax.ShapeDtypeStruct((width, width), F32),
        in_specs=[VMEM] * len(operands),
        out_specs=VMEM,
        input_output_aliases={} if partial is None else {len(pieces): 0},
        compiler_params=SMALL,
        cost_estimate=pl.CostEstimate(
            flops=2 * total * width * width, bytes_accessed=8 * width * width, transcendentals=0),
        name="partial_gram",
    )(*operands)


def dispatch(offsets, experts_of, ids, rows):
    top, tokens = ids.shape
    return pl.pallas_call(
        functools.partial(dispatch_kernel, offsets, experts_of),
        out_shape=[jax.ShapeDtypeStruct((tokens, rows.shape[1]), rows.dtype)] * len(offsets),
        in_specs=[VMEM, VMEM],
        out_specs=[VMEM] * len(offsets),
        compiler_params=SMALL,
        cost_estimate=pl.CostEstimate(
            flops=2 * 16 * top * tokens * rows.shape[1] * len(offsets),
            bytes_accessed=4 * tokens * top * rows.shape[1], transcendentals=0),
        name="dispatch",
    )(ids, rows)


def precondition(damping, partial, pieces, gradient, row_scale):
    width, columns = gradient.shape
    block = block_of(width)
    hbm = pl.BlockSpec(memory_space=pl.ANY)
    step = 256 if columns % 256 == 0 else 128
    return pl.pallas_call(
        functools.partial(factor_kernel, block, float(row_scale), len(pieces)),
        out_shape=jax.ShapeDtypeStruct((width, columns), BF16),
        in_specs=[pl.BlockSpec(memory_space=pltpu.SMEM)] + [VMEM] * (1 + len(pieces)) + [hbm],
        out_specs=hbm,
        scratch_shapes=[
            pltpu.VMEM((width, width), F32),
            pltpu.VMEM((width, width), BF16),
            pltpu.VMEM((width, columns), BF16),
            pltpu.VMEM((width, columns), BF16),
            pltpu.VMEM((2 * block, block), F32),
            pltpu.SemaphoreType.DMA,
            pltpu.SemaphoreType.DMA((columns // step,)),
        ],
        compiler_params=BIG,
        name="precondition",
    )(damping, partial, *pieces, gradient)


def swap(rows):
    return lax.ppermute(rows, "col", [(0, 1), (1, 0)])


def by_all_to_all(out_grads, expert_ids, capacity):
    hidden_width = out_grads.shape[-1]
    groups = lax.axis_size("expert")
    flat_ids = expert_ids.reshape(-1)
    onehot = (flat_ids[:, None] == jnp.arange(groups, dtype=jnp.int32)[None, :]).astype(jnp.int32)
    before = jnp.cumsum(onehot, axis=0) - onehot
    slot_index = jnp.sum(before * onehot, axis=1)
    target = flat_ids * capacity + slot_index
    outgoing = (
        jnp.zeros((groups * capacity, hidden_width), out_grads.dtype)
        .at[target]
        .set(out_grads.reshape(-1, hidden_width))
    )
    arrived = lax.all_to_all(
        outgoing.reshape(groups, capacity, hidden_width),
        "expert", split_axis=0, concat_axis=0, tiled=True,
    ).reshape(groups * capacity, hidden_width)
    half = arrived.shape[0] // 2
    other = swap(arrived)
    return partial_gram([arrived[:half], other[:half]]), [arrived[half:], other[half:]]


def by_permutes(out_grads, expert_ids):
    hidden_width = out_grads.shape[-1]
    groups = lax.axis_size("expert")
    rows, ids = out_grads.reshape(-1, hidden_width), expert_ids.T
    half = groups // 2

    def partner(me, offset):
        return me ^ offset

    def send(piece, offset):
        return lax.ppermute(piece, "expert", [(i, i ^ offset) for i in range(groups)])

    far = dispatch(tuple(range(half, groups)), partner, ids, rows)
    far = [send(piece, half + n) for n, piece in enumerate(far)]
    near = dispatch(tuple(range(half)), partner, ids, rows)
    near = [near[0]] + [send(piece, n) for n, piece in enumerate(near) if n]
    near = jnp.concatenate(near, axis=0)
    partial = partial_gram([near, swap(near)])
    cut = half // 2
    first = jnp.concatenate(far[:cut], axis=0)
    partial = partial_gram([first, swap(first)], partial)
    last = []
    for piece in far[cut:]:
        last += [piece, swap(piece)]
    return partial, last


def on_device(out_grads, expert_ids, damping, expert_grad):
    tokens_here, top_count, _ = out_grads.shape
    groups = lax.axis_size("expert")
    replicas = lax.axis_size("col")
    row_scale = tokens_here * top_count * replicas
    capacity = min(tokens_here, max(2, 2 * tokens_here * top_count // groups))
    if capacity == tokens_here and groups & (groups - 1) == 0 and groups >= 4:
        partial, last = by_permutes(out_grads, expert_ids)
    else:
        partial, last = by_all_to_all(out_grads, expert_ids, capacity)
    return precondition(damping, partial, last, expert_grad[0], row_scale)[None]


def solution(mesh):
    in_specs = (
        P(("expert", "col"), None, None),
        P(("expert", "col"), None),
        P("expert"),
        P("expert", None, "col"),
    )
    out_specs = P("expert", None, "col")
    return jax.shard_map(
        on_device, mesh=mesh, in_specs=in_specs, out_specs=out_specs, check_vma=False
    )
```
